256 devices in a mesh: rep: 32 (over y, x, core), tp: 8 (over z).
Axes of the slice: x: 4, y: 4, z: 8, core: 2. Of those that a mesh axis runs over, the one named last changes fastest.
Arguments:
- queries: bfloat16 [8192, 4096], P('rep', 'tp'), may hold values from -120 to 120
- keys_new: bfloat16 [8192, 1024], P('rep', 'tp'), may hold values from -7 to 7
- values_new: bfloat16 [8192, 1024], P('rep', 'tp'), may hold values from -6 to 6
- caches: bfloat16 [64, 2, 4096, 1024], P('rep', None, None, 'tp'), may hold values from -6 to 6
- lengths: int32 [32, 2], replicated, may hold values from 128 to 4096, as said below
- moving: int32 [32], replicated, may hold values from 0 to 1
- destination: int32 [32], replicated, may hold values from 0 to 31, each once
- out_weight: bfloat16 [4096, 4096], P('tp'), may hold values from -0.09375 to 0.09375
Outputs:
- mixed: bfloat16 [8192, 4096], P('rep', 'tp')
- held_cache: bfloat16 [64, 2, 4096, 1024], P('rep', None, None, 'tp')
The draws below stay inside these ranges and needn't reach their ends.
Inputs may be any that keep to these rules, and one draw needn't show every extreme that they name: `lengths`: multiples of 128; in every draw some slot holds 4096 and some 128. `destination`: each replica receives exactly one failing candidate; it takes the slot that its own failing candidate leaves.
All inputs are finite; a program needn't handle non-finite values.
Results may differ from the reference program's by a relative error of at most 0.014.
Values may be sent and summed in bfloat16 or wider, within the bound.
No kernel may reach another device: no remote copies, remote signals or barrier semaphores. Data moves between devices by JAX's collectives and lax.ppermute only.
A program may use at most 64 MiB of HBM per device.

```python
import jax
import jax.numpy as jnp
from jax import lax

HEADS = 32
KV_HEADS = 8
HEAD = 128
OUT = 4096
SPAN = 128
SLOTS = 2
CACHE = 4096
ROWS = 8192
N_REP = 32


def fresh_keys(key):
    base = jax.random.normal(jax.random.fold_in(key, 7), (ROWS, KV_HEADS, HEAD), jnp.float32)
    return jnp.clip(base, -6.0, 6.0)


def draw_keys_new(key, part):
    base = fresh_keys(key)
    return base.reshape(ROWS, KV_HEADS * HEAD).astype(jnp.bfloat16)


def draw_queries(key, part):
    base = jnp.clip(jax.random.normal(jax.random.fold_in(key, 11), (ROWS, HEADS, HEAD), jnp.float32), -6.0, 6.0)
    return base.reshape(ROWS, HEADS * HEAD).astype(jnp.bfloat16)


def draw_lengths(key, part):
    blocks = jax.random.randint(jax.random.fold_in(key, 3), (N_REP * SLOTS,), 1, CACHE // 128 + 1)
    picked = jax.random.permutation(jax.random.fold_in(key, 5), N_REP * SLOTS)
    blocks = blocks.at[picked[0]].set(CACHE // 128)
    blocks = blocks.at[picked[1]].set(1)
    return (blocks * 128).reshape(N_REP, SLOTS).astype(jnp.int32)


def with_ends(values, stream_key, smallest, high):
    spot = [jax.random.randint(jax.random.fold_in(stream_key, axis), (), 0, length) for axis, length in enumerate(values.shape)]
    longest = values.shape.index(max(values.shape))
    beside = spot[:longest] + [(spot[longest] + 1) % values.shape[longest]] + spot[longest + 1:]
    return values.at[tuple(spot)].set(smallest).at[tuple(beside)].set(high)


def level_of(own_key, extent, pieces, least, top_value):
    def one(dim, shards_of):
        heights = jax.random.uniform(jax.random.fold_in(jax.random.fold_in(own_key, 6), dim), (shards_of,), jnp.float32, least / len(pieces), top_value / len(pieces))
        return jnp.repeat(jnp.exp(heights), extent[dim] // shards_of).reshape((-1,) + (1,) * (len(extent) - dim - 1))

    gain = one(*pieces[0])
    for cut in pieces[1:]:
        gain = gain * one(*cut)
    return gain


def gaussian(rng, dims, deviation, reach, pieces=(), kind=jnp.bfloat16):
    level = level_of(rng, dims, pieces, -0.22, 0.18) if pieces else 1.0
    drawn = jax.random.normal(rng, dims, jnp.float32) * deviation * level
    return jnp.minimum(jnp.maximum(drawn, -reach), reach).astype(kind)


def setup_inputs(seed: int = 0) -> dict:
    streams_of = jax.random.split(jax.random.key(seed), 9)
    queries = draw_queries(jax.random.fold_in(streams_of[8], 71), 0)
    keys_new = draw_keys_new(jax.random.fold_in(streams_of[8], 71), 0)
    values_new = gaussian(streams_of[2], (ROWS, KV_HEADS * HEAD), 1.0, 6.0, ((0, 32), (1, 8)))
    caches = gaussian(streams_of[3], (N_REP * SLOTS, 2, CACHE, KV_HEADS * HEAD), 1.0, 6.0, ((0, 32), (3, 8)))
    lengths = draw_lengths(jax.random.fold_in(streams_of[8], 71), 0)
    moving = with_ends(jax.random.randint(streams_of[5], (N_REP,), 0, SLOTS), jax.random.fold_in(streams_of[5], 1), 0, SLOTS - 1).astype(jnp.int32)
    destination = jax.random.permutation(streams_of[6], N_REP).astype(jnp.int32)
    out_weight = gaussian(streams_of[7], (HEADS * HEAD, OUT), (HEADS * HEAD) ** -0.5, 0.09375, ((0, 8),))
    return {"queries": queries, "keys_new": keys_new, "values_new": values_new, "caches": caches, "lengths": lengths, "moving": moving, "destination": destination, "out_weight": out_weight}


masked_score = -1e30
key_block_rows = 512


def product(form, left, right):
    return jnp.einsum(form, left.astype(jnp.float32), right.astype(jnp.float32))


def attend(query_slot, key_cache, value_cache, length, keys_fresh, values_fresh, block_count):
    span_rows = query_slot.shape[0]
    kv_count = key_cache.shape[1] // HEAD
    group_size = query_slot.shape[1] // (HEAD * kv_count)
    grouped = query_slot.reshape(span_rows, kv_count, group_size, HEAD).transpose(1, 2, 0, 3)
    grouped = grouped.reshape(kv_count, group_size * span_rows, HEAD)
    scale = HEAD ** -0.5
    token_of_row = jnp.arange(group_size * span_rows, dtype=jnp.int32) % span_rows

    def absorb(running, key_block, value_block, visible):
        row_max, row_total, weighted = running
        scores = product('gqd,kgd->gqk', grouped, key_block) * scale
        scores = jnp.where(visible, scores, masked_score)
        new_max = jnp.maximum(row_max, jnp.max(scores, axis=2))
        rescale = jnp.exp(row_max - new_max)
        weights_block = jnp.where(visible, jnp.exp(scores - new_max[:, :, None]), 0.0)
        row_total = row_total * rescale + jnp.sum(weights_block, axis=2)
        rounded = lax.optimization_barrier(weights_block.astype(jnp.bfloat16))
        weighted = weighted * rescale[:, :, None] + product('gqk,kgd->gqd', rounded, value_block)
        return new_max, row_total, weighted

    def cache_step(block_index, running):
        start = block_index * key_block_rows
        key_block = lax.dynamic_slice_in_dim(key_cache, start, key_block_rows, 0).reshape(key_block_rows, kv_count, HEAD)
        value_block = lax.dynamic_slice_in_dim(value_cache, start, key_block_rows, 0).reshape(key_block_rows, kv_count, HEAD)
        visible = (start + jnp.arange(key_block_rows, dtype=jnp.int32) < length)[None, None, :]
        return absorb(running, key_block, value_block, visible)

    rows_all = group_size * span_rows
    initial = (jnp.full((kv_count, rows_all), masked_score, jnp.float32),
               jnp.zeros((kv_count, rows_all), jnp.float32),
               jnp.zeros((kv_count, rows_all, HEAD), jnp.float32))
    running = lax.fori_loop(0, block_count, cache_step, initial)
    visible = (jnp.arange(span_rows, dtype=jnp.int32)[None, :] <= token_of_row[:, None])[None]
    running = absorb(running, keys_fresh.reshape(span_rows, kv_count, HEAD),
                     values_fresh.reshape(span_rows, kv_count, HEAD), visible)
    result = running[2] / running[1][:, :, None]
    result = result.reshape(kv_count, group_size, span_rows, HEAD).transpose(2, 0, 1, 3)
    return result.reshape(span_rows, kv_count * group_size * HEAD).astype(jnp.bfloat16)


def reference(queries, keys_new, values_new, caches, lengths, moving, destination, out_weight):
    source_of = jnp.argsort(destination).astype(jnp.int32)
    flat_lengths = lengths.reshape(-1)
    slot_indices = jnp.arange(N_REP * SLOTS, dtype=jnp.int32)
    replica_of = slot_indices // SLOTS
    number_of = slot_indices % SLOTS
    anchor_of = source_of[replica_of]
    taken_all = jnp.where(number_of == moving[replica_of], anchor_of * SLOTS + moving[anchor_of],
                          slot_indices).astype(jnp.int32)
    held_cache = jnp.take(caches, taken_all, axis=0)

    def per_slot(slot_index):
        taken = taken_all[slot_index]
        cache_slot = lax.dynamic_index_in_dim(held_cache, slot_index, 0, keepdims=False)
        length = flat_lengths[taken]
        start = (slot_index * SPAN).astype(jnp.int32)
        query_slot = lax.dynamic_slice_in_dim(queries, start, SPAN, 0)
        keys_fresh = lax.dynamic_slice_in_dim(keys_new, start, SPAN, 0)
        values_fresh = lax.dynamic_slice_in_dim(values_new, start, SPAN, 0)
        return attend(query_slot, cache_slot[0], cache_slot[1], length, keys_fresh, values_fresh, CACHE // key_block_rows)

    attended = lax.map(per_slot, slot_indices)
    attended = attended.reshape(N_REP * SLOTS * SPAN, HEADS * HEAD)
    mixed = jnp.dot(attended, out_weight, preferred_element_type=jnp.float32).astype(jnp.bfloat16)
    return (mixed, held_cache)
```

```python
import functools

import jax
import jax.numpy as jnp
from jax import lax
from jax.experimental import pallas as pl
from jax.experimental.pallas import tpu as pltpu
from jax.sharding import Mesh
from jax.sharding import PartitionSpec as P

HEAD = 128
REP = ("rep_0", "rep_1", "rep_2")
LOG2E = 1.4426950408889634
MASKED = -1e30
CHUNK = 512


def slot_kernel(group, chunks, peers, scalars, q_ref, kn_ref, vn_ref, cache, weight, *rest):
    held = rest[-peers - 11]
    blocks = rest[-peers - 10 : -10]
    kbuf, vbuf, wbuf, mbuf, lbuf, acc, in_sem, out_sem, w_sem, obuf = rest[-10:]
    source, target, length, me = scalars[0], scalars[1], scalars[2], scalars[3]
    span = q_ref.shape[0]
    rows = chunks * CHUNK

    def load(c):
        piece = pl.ds(c * CHUNK, CHUNK)
        return (
            pltpu.make_async_copy(cache.at[source, 0, piece], kbuf.at[piece], in_sem.at[0, c]),
            pltpu.make_async_copy(cache.at[source, 1, piece], vbuf.at[piece], in_sem.at[1, c]),
        )

    def save(c):
        piece = pl.ds(c * CHUNK, CHUNK)
        return (
            pltpu.make_async_copy(kbuf.at[piece], held.at[target, 0, piece], out_sem.at[0, c]),
            pltpu.make_async_copy(vbuf.at[piece], held.at[target, 1, piece], out_sem.at[1, c]),
        )

    for c in range(chunks):
        for copy in load(c):
            copy.start()
    weight_copy = pltpu.make_async_copy(weight, wbuf, w_sem)
    weight_copy.start()

    factor = HEAD**-0.5 * LOG2E
    lanes = lambda h: pl.ds(h * HEAD, HEAD)
    contract = (((1,), (1,)), ((), ()))

    keys = kn_ref[...]
    values = vn_ref[...]
    row = lax.broadcasted_iota(jnp.int32, (span, span), 0)
    col = lax.broadcasted_iota(jnp.int32, (span, span), 1)
    for h in range(group):
        scores = lax.dot_general(q_ref[:, lanes(h)], keys, contract, preferred_element_type=jnp.float32)
        scores = jnp.where(col <= row, scores * factor, MASKED)
        top = jnp.max(scores, axis=1, keepdims=True)
        weights = jnp.exp2(scores - top)
        mbuf[h] = jnp.broadcast_to(top, (span, HEAD))
        lbuf[h] = jnp.broadcast_to(jnp.sum(weights, axis=1, keepdims=True), (span, HEAD))
        acc[h] = jnp.dot(weights.astype(jnp.bfloat16), values, preferred_element_type=jnp.float32)

    def step(c, _):
        for copy in load(c):
            copy.wait()
        for copy in save(c):
            copy.start()

        @pl.when(c * CHUNK < length)
        def _():
            piece = pl.ds(pl.multiple_of(c * CHUNK, CHUNK), CHUNK)
            keys = kbuf[piece, :]
            values = vbuf[piece, :]
            seen = lax.broadcasted_iota(jnp.int32, (span, CHUNK), 1) < length - c * CHUNK
            for h in range(group):
                scores = lax.dot_general(
                    q_ref[:, lanes(h)], keys, contract, preferred_element_type=jnp.float32
                )
                scores = jnp.where(seen, scores * factor, MASKED)
                before = mbuf[h]
                top = jnp.maximum(before, jnp.max(scores, axis=1, keepdims=True))
                shrink = jnp.exp2(before - top)
                weights = jnp.exp2(scores - top[:, :1])
                mbuf[h] = top
                lbuf[h] = lbuf[h] * shrink + jnp.sum(weights, axis=1, keepdims=True)
                acc[h] = acc[h] * shrink + jnp.dot(
                    weights.astype(jnp.bfloat16), values, preferred_element_type=jnp.float32
                )

        return 0

    lax.fori_loop(0, chunks, step, 0)
    for h in range(group):
        obuf[:, lanes(h)] = (acc[h] / lbuf[h]).astype(jnp.bfloat16)
    weight_copy.wait()
    width = wbuf.shape[1] // peers
    for k in range(peers):
        owner = lax.rem(me + k, peers)
        columns = pl.ds(pl.multiple_of(owner * width, width), width)
        blocks[k][...] = jnp.dot(
            obuf[...], wbuf[:, columns], preferred_element_type=jnp.float32
        ).astype(jnp.bfloat16)
    for c in range(chunks):
        for copy in save(c):
            copy.wait()


def run_slot(scalars, span, queries, keys_new, values_new, cache, weight, peers, held=None):
    group = queries.shape[1] // HEAD
    rows = cache.shape[2]
    chunks = rows // CHUNK
    width = weight.shape[1] // peers
    slots = queries.shape[0] // span
    anywhere = pl.BlockSpec(memory_space=pl.ANY)
    operands = [queries, keys_new, values_new, cache, weight]
    in_specs = [
        pl.BlockSpec((span, queries.shape[1]), lambda i, s: (s[4], 0)),
        pl.BlockSpec((span, HEAD), lambda i, s: (s[4], 0)),
        pl.BlockSpec((span, HEAD), lambda i, s: (s[4], 0)),
        anywhere,
        anywhere,
    ]
    aliases = {}
    if held is not None:
        operands.append(held)
        in_specs.append(anywhere)
        aliases = {6: 0}
    flops = 4 * group * span * HEAD * (rows + span) + 2 * span * weight.shape[0] * weight.shape[1]
    return pl.pallas_call(
        functools.partial(slot_kernel, group, chunks, peers),
        out_shape=[jax.ShapeDtypeStruct((slots, 2, rows, HEAD), cache.dtype)]
        + [jax.ShapeDtypeStruct((span, width), jnp.bfloat16)] * peers,
        grid_spec=pltpu.PrefetchScalarGridSpec(
            num_scalar_prefetch=1,
            grid=(1,),
            in_specs=in_specs,
            out_specs=[anywhere] + [pl.BlockSpec((span, width), lambda i, s: (0, 0))] * peers,
            scratch_shapes=[
                pltpu.VMEM((rows, HEAD), jnp.bfloat16),
                pltpu.VMEM((rows, HEAD), jnp.bfloat16),
                pltpu.VMEM(weight.shape, jnp.bfloat16),
                pltpu.VMEM((group, span, HEAD), jnp.float32),
                pltpu.VMEM((group, span, HEAD), jnp.float32),
                pltpu.VMEM((group, span, HEAD), jnp.float32),
                pltpu.SemaphoreType.DMA((2, chunks)),
                pltpu.SemaphoreType.DMA((2, chunks)),
                pltpu.SemaphoreType.DMA,
                pltpu.VMEM((span, group * HEAD), jnp.bfloat16),
            ],
        ),
        input_output_aliases=aliases,
        compiler_params=pltpu.CompilerParams(vmem_limit_bytes=24 * 2**20),
        cost_estimate=pl.CostEstimate(
            flops=flops,
            bytes_accessed=8 * rows * HEAD + weight.size * 2,
            transcendentals=group * span * rows,
        ),
        name="slot",
    )(scalars, *operands)


def sum_over_tp(blocks):
    peers = len(blocks)
    total = blocks[0].astype(jnp.float32)
    for k in range(1, peers):
        arrived = lax.ppermute(blocks[k], "tp", [(i, (i + k) % peers) for i in range(peers)])
        total = total + arrived.astype(jnp.float32)
    return total.astype(jnp.bfloat16)


def on_device(queries, keys_new, values_new, caches, lengths, moving, destination, out_weight):
    replicas = lax.axis_size(REP)
    peers = lax.axis_size("tp")
    own_index = lax.axis_index(REP)
    me = lax.axis_index("tp").astype(jnp.int32)
    slots, _, rows, _ = caches.shape
    span = queries.shape[0] // slots
    order = jnp.arange(replicas, dtype=jnp.int32)
    source_of = jnp.sum(jnp.where(destination[None, :] == order[:, None], order[None, :], 0), axis=1)
    leaving = moving[own_index]
    staying = 1 - leaving
    anchor = source_of[own_index]

    sent = lax.dynamic_index_in_dim(caches, leaving, 0, keepdims=False)
    sent = sent.reshape(replicas, 2 * rows // replicas, HEAD)
    spread = lax.all_to_all(sent, REP, 0, 0, tiled=True)
    ordered = spread.at[source_of].get(mode="promise_in_bounds")
    arrived = lax.all_to_all(ordered, REP, 0, 0, tiled=True)
    arrived = arrived.reshape(1, 2, rows, HEAD)

    shared = (queries, keys_new, values_new)
    held, *stay_blocks = run_slot(
        jnp.stack([staying, staying, lengths[own_index, staying], me, staying]),
        span, *shared, caches, out_weight, peers,
    )
    stay_mixed = sum_over_tp(stay_blocks)
    held, *move_blocks = run_slot(
        jnp.stack([jnp.zeros_like(leaving), leaving, lengths[anchor, moving[anchor]], me, leaving]),
        span, *shared, arrived, out_weight, peers, held,
    )
    move_mixed = sum_over_tp(move_blocks)
    first = jnp.where(leaving == 0, move_mixed, stay_mixed)
    second = jnp.where(leaving == 0, stay_mixed, move_mixed)
    return jnp.concatenate([first, second], axis=0), held


def solution(mesh):
    split = Mesh(mesh.devices.reshape(4, 4, 2, mesh.shape["tp"]), REP + ("tp",))
    return jax.shard_map(
        on_device,
        mesh=split,
        in_specs=(
            P(REP, "tp"),
            P(REP, "tp"),
            P(REP, "tp"),
            P(REP, None, None, "tp"),
            P(),
            P(),
            P(),
            P("tp", None),
        ),
        out_specs=(P(REP, "tp"), P(REP, None, None, "tp")),
        check_vma=False,
    )
```

```python
import functools

import jax
import jax.numpy as jnp
from jax import lax
from jax.experimental import pallas as pl
from jax.experimental.pallas import tpu as pltpu
from jax.sharding import Mesh
from jax.sharding import PartitionSpec as P

HEAD = 128
REP = ("rep_0", "rep_1", "rep_2")
LOG2E = 1.4426950408889634
MASKED = -1e30
CHUNK = 2048


def place():
    return lax.axis_index(REP).astype(jnp.int32), lax.axis_index("tp").astype(jnp.int32)


def pick_kernel(moving, caches, sent, sems):
    own, _ = place()
    leaving = moving[own]
    pieces = sems.shape[0]
    rows = sent.shape[0] // pieces

    def copy(i):
        piece = pl.ds(i * rows, rows)
        return pltpu.make_async_copy(caches.at[leaving, piece], sent.at[piece], sems.at[i])

    for i in range(pieces):
        copy(i).start()
    for i in range(pieces):
        copy(i).wait()


def pick(moving, caches):
    slots, _, rows, _ = caches.shape
    return pl.pallas_call(
        pick_kernel,
        out_shape=jax.ShapeDtypeStruct((2 * rows, HEAD), caches.dtype),
        in_specs=[pl.BlockSpec(memory_space=pltpu.SMEM), pl.BlockSpec(memory_space=pltpu.HBM)],
        out_specs=pl.BlockSpec(memory_space=pltpu.VMEM),
        scratch_shapes=[pltpu.SemaphoreType.DMA((4,))],
        compiler_params=pltpu.CompilerParams(vmem_limit_bytes=36 * 2**20),
        cost_estimate=pl.CostEstimate(flops=0, bytes_accessed=8 * rows * HEAD, transcendentals=0),
        name="pick",
    )(moving, pltpu.with_memory_space_constraint(caches.reshape(slots, 2 * rows, HEAD), pltpu.HBM))


def slot_kernel(arrived, group, chunk, parts, lengths, moving, destination, queries, keys_new, values_new, cache, weight, *rest):
    scratch = 13
    if arrived:
        rest = rest[1:]
    held = rest[0]
    outs = rest[1:-scratch]
    (qbuf, knbuf, vnbuf, kbuf, vbuf, wbuf, top_ref, sum_ref, acc, obuf, in_sem, out_sem, sems) = rest[-scratch:]
    own, me = place()
    replicas = destination.shape[0]
    chunks = kbuf.shape[0] // chunk
    span = qbuf.shape[0]
    peers = len(parts)
    leaving = moving[own]
    if arrived:
        source, target = 0, leaving
        anchor = jnp.int32(0)
        for r in range(replicas):
            anchor = jnp.where(destination[r] == own, r, anchor)
        length = lengths[anchor, moving[anchor]]
    else:
        source = target = 1 - leaving
        length = lengths[own, target]

    def load(c):
        piece = pl.ds(c * chunk, chunk)
        return (
            pltpu.make_async_copy(cache.at[source, 0, piece], kbuf.at[piece], in_sem.at[0, c]),
            pltpu.make_async_copy(cache.at[source, 1, piece], vbuf.at[piece], in_sem.at[1, c]),
        )

    def save(c):
        piece = pl.ds(c * chunk, chunk)
        return (
            pltpu.make_async_copy(kbuf.at[piece], held.at[target, 0, piece], out_sem.at[0, c]),
            pltpu.make_async_copy(vbuf.at[piece], held.at[target, 1, piece], out_sem.at[1, c]),
        )

    own_rows = pl.ds(pl.multiple_of(target * span, span), span)
    small = (
        pltpu.make_async_copy(queries.at[own_rows], qbuf, sems.at[0]),
        pltpu.make_async_copy(keys_new.at[own_rows], knbuf, sems.at[1]),
        pltpu.make_async_copy(values_new.at[own_rows], vnbuf, sems.at[2]),
    )
    weight_copy = pltpu.make_async_copy(weight, wbuf, sems.at[3])
    for copy in small:
        copy.start()
    for c in range(chunks):
        for copy in load(c):
            copy.start()
    weight_copy.start()
    for copy in small:
        copy.wait()

    factor = HEAD**-0.5 * LOG2E
    rows = group * span
    over_head = (((1,), (1,)), ((), ()))
    over_keys = (((0,), (0,)), ((), ()))
    grouped = jnp.concatenate([qbuf[:, pl.ds(h * HEAD, HEAD)] for h in range(group)], axis=0)
    key_at = lax.broadcasted_iota(jnp.int32, (span, rows), 0)
    row_at = lax.rem(lax.broadcasted_iota(jnp.int32, (span, rows), 1), span)
    scores = lax.dot_general(knbuf[...], grouped, over_head, preferred_element_type=jnp.float32)
    scores = jnp.where(key_at <= row_at, scores * factor, MASKED)
    top = jnp.max(scores, axis=0, keepdims=True)
    weights = jnp.exp2(scores - top)
    top_ref[...] = top
    sum_ref[...] = jnp.sum(weights, axis=0, keepdims=True)
    acc[...] = lax.dot_general(
        vnbuf[...], weights.astype(jnp.bfloat16), over_keys, preferred_element_type=jnp.float32
    )

    def step(c, _):
        for copy in load(c):
            copy.wait()
        for copy in save(c):
            copy.start()

        @pl.when(c * chunk < length)
        def _():
            piece = pl.ds(pl.multiple_of(c * chunk, chunk), chunk)
            scores = lax.dot_general(kbuf[piece, :], grouped, over_head, preferred_element_type=jnp.float32)
            seen = lax.broadcasted_iota(jnp.int32, (chunk, rows), 0) < length - c * chunk
            scores = jnp.where(seen, scores * factor, MASKED)
            before = top_ref[...]
            top = jnp.maximum(before, jnp.max(scores, axis=0, keepdims=True))
            shrink = jnp.exp2(before - top)
            weights = jnp.exp2(scores - top)
            top_ref[...] = top
            sum_ref[...] = sum_ref[...] * shrink + jnp.sum(weights, axis=0, keepdims=True)
            acc[...] = acc[...] * shrink + lax.dot_general(
                vbuf[piece, :], weights.astype(jnp.bfloat16), over_keys, preferred_element_type=jnp.float32
            )

        return 0

    lax.fori_loop(0, chunks, step, 0)
    result = acc[...] / sum_ref[...]
    for h in range(group):
        obuf[:, pl.ds(h * HEAD, HEAD)] = result[:, h * span : (h + 1) * span].T.astype(jnp.bfloat16)
    weight_copy.wait()
    width = wbuf.shape[1] // peers
    out = 0
    for k in range(peers):
        columns = pl.ds(pl.multiple_of(lax.rem(me + k, peers) * width, width), width)
        block = jnp.dot(obuf[...], wbuf[:, columns], preferred_element_type=jnp.float32)
        block = block.astype(jnp.bfloat16)
        height = span // parts[k]
        for part in range(parts[k]):
            outs[out][...] = block[part * height : (part + 1) * height]
            out += 1
    for c in range(chunks):
        for copy in save(c):
            copy.wait()


def run_slot(lengths, moving, destination, queries, keys_new, values_new, cache, weight, parts, held=None):
    span = queries.shape[0] // lengths.shape[1]
    slots = lengths.shape[1]
    group = queries.shape[1] // HEAD
    rows = cache.shape[2]
    peers = len(parts)
    chunks = rows // CHUNK
    width = weight.shape[1] // peers
    smem = pl.BlockSpec(memory_space=pltpu.SMEM)
    vmem = pl.BlockSpec(memory_space=pltpu.VMEM)
    hbm = pl.BlockSpec(memory_space=pltpu.HBM)
    weight = pltpu.with_memory_space_constraint(weight, pltpu.HBM)
    if held is None:
        cache = pltpu.with_memory_space_constraint(cache, pltpu.HBM)
    operands = [lengths, moving, destination, queries, keys_new, values_new, cache, weight]
    in_specs = [smem] * 3 + [pl.BlockSpec(memory_space=pl.ANY)] * 3
    in_specs += [hbm if held is None else pl.BlockSpec(memory_space=pl.ANY), hbm]
    aliases = {}
    if held is not None:
        operands.append(held)
        in_specs.append(hbm)
        aliases = {8: 0}
    shapes = [jax.ShapeDtypeStruct((slots, 2, rows, HEAD), cache.dtype)]
    for count in parts:
        shapes += [jax.ShapeDtypeStruct((span // count, width), jnp.bfloat16)] * count
    flops = 4 * group * span * HEAD * (rows + span) + 2 * span * weight.shape[0] * weight.shape[1]
    return pl.pallas_call(
        functools.partial(slot_kernel, held is not None, group, CHUNK, parts),
        out_shape=shapes,
        in_specs=in_specs,
        out_specs=[hbm] + [vmem] * (len(shapes) - 1),
        scratch_shapes=[
            pltpu.VMEM((span, group * HEAD), jnp.bfloat16),
            pltpu.VMEM((span, HEAD), jnp.bfloat16),
            pltpu.VMEM((span, HEAD), jnp.bfloat16),
            pltpu.VMEM((rows, HEAD), jnp.bfloat16),
            pltpu.VMEM((rows, HEAD), jnp.bfloat16),
            pltpu.VMEM(weight.shape, jnp.bfloat16),
            pltpu.VMEM((1, group * span), jnp.float32),
            pltpu.VMEM((1, group * span), jnp.float32),
            pltpu.VMEM((HEAD, group * span), jnp.float32),
            pltpu.VMEM((span, group * HEAD), jnp.bfloat16),
            pltpu.SemaphoreType.DMA((2, chunks)),
            pltpu.SemaphoreType.DMA((2, chunks)),
            pltpu.SemaphoreType.DMA((4,)),
        ],
        input_output_aliases=aliases,
        compiler_params=pltpu.CompilerParams(vmem_limit_bytes=36 * 2**20),
        cost_estimate=pl.CostEstimate(
            flops=flops,
            bytes_accessed=8 * rows * HEAD + weight.size * 2,
            transcendentals=group * span * rows,
        ),
        name="slot",
    )(*operands)


def shift(block, k):
    peers = lax.axis_size("tp")
    return lax.ppermute(block, "tp", [(i, (i + k) % peers) for i in range(peers)])


def widen(block):
    return block.astype(jnp.float32)


def sum_direct(blocks):
    total = widen(blocks[0])
    for k in range(1, len(blocks)):
        total = total + widen(shift(blocks[k], k))
    return total


def sum_in_two(blocks):
    b0, b1, b2, b3, b4_low, b4_high, b5, b6, b7 = blocks
    low = shift(b4_low, 2)
    high = shift(b4_high, -2)
    right = shift(b3, 1)
    left = shift(b5, -1)
    one = shift(b1, 1)
    seven = shift(b7, -1)
    half = low.shape[0]
    none = jnp.zeros_like(low)
    right = widen(b2) + widen(right) + widen(jnp.concatenate([low, none]))
    left = widen(b6) + widen(left) + widen(jnp.concatenate([none, high]))
    two = shift(right.astype(jnp.bfloat16), 2)
    six = shift(left.astype(jnp.bfloat16), -2)
    return widen(b0) + widen(one) + widen(seven) + widen(two) + widen(six)


def on_device(queries, keys_new, values_new, caches, lengths, moving, destination, out_weight):
    replicas = lax.axis_size(REP)
    peers = lax.axis_size("tp")
    slots, _, rows, _ = caches.shape
    span = queries.shape[0] // slots
    order = jnp.arange(replicas, dtype=jnp.int32)
    source_of = jnp.sum(jnp.where(destination[None, :] == order[:, None], order[None, :], 0), axis=1)
    small = (lengths, moving, destination, queries, keys_new, values_new)

    sent = pick(moving, caches).reshape(replicas, 2 * rows // replicas, HEAD)
    spread = lax.all_to_all(sent, REP, 0, 0, tiled=True)
    held, *stay = run_slot(*small, caches, out_weight, (1,) * peers)
    spread, _ = lax.optimization_barrier((spread, stay[0]))
    ordered = spread.at[source_of].get(mode="promise_in_bounds")
    arrived = lax.all_to_all(ordered, REP, 0, 0, tiled=True)
    stay_mixed = sum_direct(stay).astype(jnp.bfloat16)

    arrived = arrived.reshape(1, 2, rows, HEAD)
    held, *move = run_slot(*small, arrived, out_weight, (1, 1, 1, 1, 2, 1, 1, 1), held)
    move_mixed = sum_in_two(move).astype(jnp.bfloat16)
    leaving = moving[lax.axis_index(REP)]
    own = lax.broadcasted_iota(jnp.int32, (slots, 1, 1), 0) == leaving
    mixed = jnp.where(own, move_mixed[None], stay_mixed[None])
    return mixed.reshape(slots * span, -1), held


def solution(mesh):
    split = Mesh(mesh.devices.reshape(4, 4, 2, mesh.shape["tp"]), REP + ("tp",))
    return jax.shard_map(
        on_device,
        mesh=split,
        in_specs=(
            P(REP, "tp"),
            P(REP, "tp"),
            P(REP, "tp"),
            P(REP, None, None, "tp"),
            P(),
            P(),
            P(),
            P("tp", None),
        ),
        out_specs=(P(REP, "tp"), P(REP, None, None, "tp")),
        check_vma=False,
    )
```

```python
import functools

import jax
import jax.numpy as jnp
from jax import lax
from jax.experimental import pallas as pl
from jax.experimental.pallas import tpu as pltpu
from jax.sharding import Mesh
from jax.sharding import PartitionSpec as P

HEAD = 128
REP = ("rep_0", "rep_1", "rep_2")
LOG2E = 1.4426950408889634
MASKED = -1e30
CHUNK = 2048


def place():
    return lax.axis_index(REP).astype(jnp.int32), lax.axis_index("tp").astype(jnp.int32)


def pick_kernel(moving, caches, sent, held, in_sems, out_sems):
    own, _ = place()
    leaving = moving[own]
    pieces = in_sems.shape[0]
    rows = sent.shape[0] // pieces

    def load(i):
        piece = pl.ds(i * rows, rows)
        return pltpu.make_async_copy(caches.at[leaving, piece], held.at[piece], in_sems.at[i])

    def save(i):
        piece = pl.ds(i * rows, rows)
        return pltpu.make_async_copy(held.at[piece], sent.at[piece], out_sems.at[i])

    for i in range(pieces):
        load(i).start()
    for i in range(pieces):
        load(i).wait()
        save(i).start()
    for i in range(pieces):
        save(i).wait()


def pick(moving, caches):
    slots, _, rows, _ = caches.shape
    hbm = pl.BlockSpec(memory_space=pltpu.HBM)
    caches = pltpu.with_memory_space_constraint(caches.reshape(slots, 2 * rows, HEAD), pltpu.HBM)
    return pl.pallas_call(
        pick_kernel,
        out_shape=jax.ShapeDtypeStruct((2 * rows, HEAD), caches.dtype),
        in_specs=[pl.BlockSpec(memory_space=pltpu.SMEM), hbm],
        out_specs=hbm,
        scratch_shapes=[
            pltpu.VMEM((2 * rows, HEAD), caches.dtype),
            pltpu.SemaphoreType.DMA((8,)),
            pltpu.SemaphoreType.DMA((8,)),
        ],
        compiler_params=pltpu.CompilerParams(vmem_limit_bytes=60 * 2**20),
        cost_estimate=pl.CostEstimate(flops=0, bytes_accessed=8 * rows * HEAD, transcendentals=0),
        name="pick",
    )(moving, caches)


def slot_kernel(arrived, group, chunk, parts, lengths, moving, destination, queries, keys_new, values_new, cache, weight, *rest):
    scratch = 13
    if arrived:
        rest = rest[1:]
    held = rest[0]
    outs = rest[1:-scratch]
    (qbuf, knbuf, vnbuf, kbuf, vbuf, wbuf, top_ref, sum_ref, acc, obuf, in_sem, out_sem, sems) = rest[-scratch:]
    own, me = place()
    replicas = destination.shape[0]
    chunks = cache.shape[2] // chunk
    span = qbuf.shape[0]
    peers = len(parts)
    leaving = moving[own]
    if arrived:
        source, target = 0, leaving
        anchor = jnp.int32(0)
        for r in range(replicas):
            anchor = jnp.where(destination[r] == own, r, anchor)
        length = lengths[anchor, moving[anchor]]
    else:
        source = target = 1 - leaving
        length = lengths[own, target]

    def load(c):
        piece = pl.ds(c * chunk, chunk)
        return (
            pltpu.make_async_copy(cache.at[source, 0, piece], kbuf.at[piece], in_sem.at[0, c]),
            pltpu.make_async_copy(cache.at[source, 1, piece], vbuf.at[piece], in_sem.at[1, c]),
        )

    def save(c):
        piece = pl.ds(c * chunk, chunk)
        return (
            pltpu.make_async_copy(kept(0, piece), held.at[target, 0, piece], out_sem.at[0, c]),
            pltpu.make_async_copy(kept(1, piece), held.at[target, 1, piece], out_sem.at[1, c]),
        )

    def kept(which, piece):
        if arrived:
            return cache.at[0, which, piece]
        return (kbuf, vbuf)[which].at[piece]

    own_rows = pl.ds(pl.multiple_of(target * span, span), span)
    small = (
        pltpu.make_async_copy(queries.at[own_rows], qbuf, sems.at[0]),
        pltpu.make_async_copy(keys_new.at[own_rows], knbuf, sems.at[1]),
        pltpu.make_async_copy(values_new.at[own_rows], vnbuf, sems.at[2]),
    )
    weight_copy = pltpu.make_async_copy(weight, wbuf, sems.at[3])
    for copy in small:
        copy.start()
    for c in range(chunks):
        for copy in save(c) if arrived else load(c):
            copy.start()
    weight_copy.start()
    for copy in small:
        copy.wait()

    factor = HEAD**-0.5 * LOG2E
    rows = group * span
    over_head = (((1,), (1,)), ((), ()))
    over_keys = (((0,), (0,)), ((), ()))
    grouped = jnp.concatenate([qbuf[:, pl.ds(h * HEAD, HEAD)] for h in range(group)], axis=0)
    key_at = lax.broadcasted_iota(jnp.int32, (span, rows), 0)
    row_at = lax.rem(lax.broadcasted_iota(jnp.int32, (span, rows), 1), span)
    scores = lax.dot_general(knbuf[...], grouped, over_head, preferred_element_type=jnp.float32)
    scores = jnp.where(key_at <= row_at, scores * factor, MASKED)
    top = jnp.max(scores, axis=0, keepdims=True)
    weights = jnp.exp2(scores - top)
    top_ref[...] = top
    sum_ref[...] = jnp.sum(weights, axis=0, keepdims=True)
    acc[...] = lax.dot_general(
        vnbuf[...], weights.astype(jnp.bfloat16), over_keys, preferred_element_type=jnp.float32
    )

    def step(c, _):
        if not arrived:
            for copy in load(c):
                copy.wait()
            for copy in save(c):
                copy.start()

        @pl.when(c * chunk < length)
        def _():
            piece = pl.ds(pl.multiple_of(c * chunk, chunk), chunk)
            scores = lax.dot_general(kept(0, piece)[...], grouped, over_head, preferred_element_type=jnp.float32)
            seen = lax.broadcasted_iota(jnp.int32, (chunk, rows), 0) < length - c * chunk
            scores = jnp.where(seen, scores * factor, MASKED)
            before = top_ref[...]
            top = jnp.maximum(before, jnp.max(scores, axis=0, keepdims=True))
            shrink = jnp.exp2(before - top)
            weights = jnp.exp2(scores - top)
            top_ref[...] = top
            sum_ref[...] = sum_ref[...] * shrink + jnp.sum(weights, axis=0, keepdims=True)
            acc[...] = acc[...] * shrink + lax.dot_general(
                kept(1, piece)[...], weights.astype(jnp.bfloat16), over_keys, preferred_element_type=jnp.float32
            )

        return 0

    lax.fori_loop(0, chunks, step, 0)
    result = acc[...] / sum_ref[...]
    for h in range(group):
        obuf[:, pl.ds(h * HEAD, HEAD)] = result[:, h * span : (h + 1) * span].T.astype(jnp.bfloat16)
    weight_copy.wait()
    width = wbuf.shape[1] // peers
    out = 0
    for k in range(peers):
        columns = pl.ds(pl.multiple_of(lax.rem(me + k, peers) * width, width), width)
        block = jnp.dot(obuf[...], wbuf[:, columns], preferred_element_type=jnp.float32)
        block = block.astype(jnp.bfloat16)
        height = span // parts[k]
        for part in range(parts[k]):
            outs[out][...] = block[part * height : (part + 1) * height]
            out += 1
    for c in range(chunks):
        for copy in save(c):
            copy.wait()


def run_slot(lengths, moving, destination, queries, keys_new, values_new, cache, weight, parts, held=None):
    span = queries.shape[0] // lengths.shape[1]
    slots = lengths.shape[1]
    group = queries.shape[1] // HEAD
    rows = cache.shape[2]
    peers = len(parts)
    chunks = rows // CHUNK
    kept = rows if held is None else 16
    width = weight.shape[1] // peers
    smem = pl.BlockSpec(memory_space=pltpu.SMEM)
    vmem = pl.BlockSpec(memory_space=pltpu.VMEM)
    hbm = pl.BlockSpec(memory_space=pltpu.HBM)
    weight = pltpu.with_memory_space_constraint(weight, pltpu.HBM)
    if held is None:
        cache = pltpu.with_memory_space_constraint(cache, pltpu.HBM)
    operands = [lengths, moving, destination, queries, keys_new, values_new, cache, weight]
    in_specs = [smem] * 3 + [pl.BlockSpec(memory_space=pl.ANY)] * 3
    in_specs += [hbm if held is None else vmem, hbm]
    aliases = {}
    if held is not None:
        operands.append(held)
        in_specs.append(hbm)
        aliases = {8: 0}
    shapes = [jax.ShapeDtypeStruct((slots, 2, rows, HEAD), cache.dtype)]
    for count in parts:
        shapes += [jax.ShapeDtypeStruct((span // count, width), jnp.bfloat16)] * count
    flops = 4 * group * span * HEAD * (rows + span) + 2 * span * weight.shape[0] * weight.shape[1]
    return pl.pallas_call(
        functools.partial(slot_kernel, held is not None, group, CHUNK, parts),
        out_shape=shapes,
        in_specs=in_specs,
        out_specs=[hbm] + [vmem] * (len(shapes) - 1),
        scratch_shapes=[
            pltpu.VMEM((span, group * HEAD), jnp.bfloat16),
            pltpu.VMEM((span, HEAD), jnp.bfloat16),
            pltpu.VMEM((span, HEAD), jnp.bfloat16),
            pltpu.VMEM((kept, HEAD), jnp.bfloat16),
            pltpu.VMEM((kept, HEAD), jnp.bfloat16),
            pltpu.VMEM(weight.shape, jnp.bfloat16),
            pltpu.VMEM((1, group * span), jnp.float32),
            pltpu.VMEM((1, group * span), jnp.float32),
            pltpu.VMEM((HEAD, group * span), jnp.float32),
            pltpu.VMEM((span, group * HEAD), jnp.bfloat16),
            pltpu.SemaphoreType.DMA((2, chunks)),
            pltpu.SemaphoreType.DMA((2, chunks)),
            pltpu.SemaphoreType.DMA((4,)),
        ],
        input_output_aliases=aliases,
        compiler_params=pltpu.CompilerParams(vmem_limit_bytes=36 * 2**20),
        cost_estimate=pl.CostEstimate(
            flops=flops,
            bytes_accessed=8 * rows * HEAD + weight.size * 2,
            transcendentals=group * span * rows,
        ),
        name="slot",
    )(*operands)


def shift(block, k):
    peers = lax.axis_size("tp")
    return lax.ppermute(block, "tp", [(i, (i + k) % peers) for i in range(peers)])


def widen(block):
    return block.astype(jnp.float32)


def sum_direct(blocks):
    total = widen(blocks[0])
    for k in range(1, len(blocks)):
        total = total + widen(shift(blocks[k], k))
    return total


def sum_in_two(blocks):
    b0, b1, b2, b3, b4_low, b4_high, b5, b6, b7 = blocks
    right = shift(b3, 1)
    left = shift(b5, -1)
    low = shift(b4_low, 2)
    high = shift(b4_high, -2)
    b1, b7, right, left = lax.optimization_barrier((b1, b7, right, left))
    one = shift(b1, 1)
    seven = shift(b7, -1)
    half = low.shape[0]
    none = jnp.zeros_like(low)
    right = widen(b2) + widen(right) + widen(jnp.concatenate([low, none]))
    left = widen(b6) + widen(left) + widen(jnp.concatenate([none, high]))
    two = shift(right.astype(jnp.bfloat16), 2)
    six = shift(left.astype(jnp.bfloat16), -2)
    return widen(b0) + widen(one) + widen(seven) + widen(two) + widen(six)


def on_device(queries, keys_new, values_new, caches, lengths, moving, destination, out_weight):
    replicas = lax.axis_size(REP)
    peers = lax.axis_size("tp")
    slots, _, rows, _ = caches.shape
    span = queries.shape[0] // slots
    order = jnp.arange(replicas, dtype=jnp.int32)
    source_of = jnp.sum(jnp.where(destination[None, :] == order[:, None], order[None, :], 0), axis=1)
    small = (lengths, moving, destination, queries, keys_new, values_new)

    sent = pick(moving, caches).reshape(replicas, 2 * rows // replicas, HEAD)
    spread = lax.all_to_all(sent, REP, 0, 0, tiled=True)
    held, *stay = run_slot(*small, caches, out_weight, (1,) * peers)
    spread, _ = lax.optimization_barrier((spread, stay[0]))
    ordered = spread.at[source_of].get(mode="promise_in_bounds")
    arrived = lax.all_to_all(ordered, REP, 0, 0, tiled=True)
    stay_mixed = sum_direct(stay).astype(jnp.bfloat16)

    leaving = moving[lax.axis_index(REP)]
    own = lax.broadcasted_iota(jnp.int32, (slots, 1, 1), 0) == leaving
    arrived, stay_mixed, own = lax.optimization_barrier((arrived, stay_mixed, own))
    arrived = arrived.reshape(1, 2, rows, HEAD)
    held, *move = run_slot(*small, arrived, out_weight, (1, 1, 1, 1, 2, 1, 1, 1), held)
    move_mixed = sum_in_two(move).astype(jnp.bfloat16)
    mixed = jnp.where(own, move_mixed[None], stay_mixed[None])
    return mixed.reshape(slots * span, -1), held


def solution(mesh):
    split = Mesh(mesh.devices.reshape(4, 4, 2, mesh.shape["tp"]), REP + ("tp",))
    return jax.shard_map(
        on_device,
        mesh=split,
        in_specs=(
            P(REP, "tp"),
            P(REP, "tp"),
            P(REP, "tp"),
            P(REP, None, None, "tp"),
            P(),
            P(),
            P(),
            P("tp", None),
        ),
        out_specs=(P(REP, "tp"), P(REP, None, None, "tp")),
        check_vma=False,
    )
```

```python
import functools

import jax
import jax.numpy as jnp
from jax import lax
from jax.experimental import pallas as pl
from jax.experimental.pallas import tpu as pltpu
from jax.sharding import Mesh
from jax.sharding import PartitionSpec as P

HEAD = 128
REP = ("rep_0", "rep_1", "rep_2")
LOG2E = 1.4426950408889634
MASKED = -1e30
CHUNK = 2048
PARTS = (1, 1, 1, 1, 2, 1, 1, 1)


def place():
    return lax.axis_index(REP).astype(jnp.int32), lax.axis_index("tp").astype(jnp.int32)


def pick_kernel(moving, caches, sent, held, in_sems, out_sems):
    own, _ = place()
    leaving = moving[own]
    pieces = in_sems.shape[0]
    rows = sent.shape[0] // pieces

    def load(i):
        piece = pl.ds(i * rows, rows)
        return pltpu.make_async_copy(caches.at[leaving, piece], held.at[piece], in_sems.at[i])

    def save(i):
        piece = pl.ds(i * rows, rows)
        return pltpu.make_async_copy(held.at[piece], sent.at[piece], out_sems.at[i])

    for i in range(pieces):
        load(i).start()
    for i in range(pieces):
        load(i).wait()
        save(i).start()
    for i in range(pieces):
        save(i).wait()


def pick(moving, caches):
    slots, _, rows, _ = caches.shape
    hbm = pl.BlockSpec(memory_space=pltpu.HBM)
    caches = pltpu.with_memory_space_constraint(caches.reshape(slots, 2 * rows, HEAD), pltpu.HBM)
    return pl.pallas_call(
        pick_kernel,
        out_shape=jax.ShapeDtypeStruct((2 * rows, HEAD), caches.dtype),
        in_specs=[pl.BlockSpec(memory_space=pltpu.SMEM), hbm],
        out_specs=hbm,
        scratch_shapes=[
            pltpu.VMEM((2 * rows, HEAD), caches.dtype),
            pltpu.SemaphoreType.DMA((8,)),
            pltpu.SemaphoreType.DMA((8,)),
        ],
        compiler_params=pltpu.CompilerParams(vmem_limit_bytes=60 * 2**20),
        cost_estimate=pl.CostEstimate(flops=0, bytes_accessed=8 * rows * HEAD, transcendentals=0),
        name="pick",
    )(moving, caches)


def slot_kernel(arrived, group, chunk, parts, lengths, moving, destination, queries, keys_new, values_new, cache, weight, *rest):
    scratch = 13
    if arrived:
        rest = rest[1:]
    held = rest[0]
    outs = rest[1:-scratch]
    (qbuf, knbuf, vnbuf, kbuf, vbuf, wbuf, top_ref, sum_ref, acc, obuf, in_sem, out_sem, sems) = rest[-scratch:]
    own, me = place()
    replicas = destination.shape[0]
    chunks = cache.shape[2] // chunk
    span = qbuf.shape[0]
    peers = len(parts)
    leaving = moving[own]
    if arrived:
        source, target = 0, leaving
        anchor = jnp.int32(0)
        for r in range(replicas):
            anchor = jnp.where(destination[r] == own, r, anchor)
        length = lengths[anchor, moving[anchor]]
    else:
        source = target = 1 - leaving
        length = lengths[own, target]

    def load(c):
        piece = pl.ds(c * chunk, chunk)
        return (
            pltpu.make_async_copy(cache.at[source, 0, piece], kbuf.at[piece], in_sem.at[0, c]),
            pltpu.make_async_copy(cache.at[source, 1, piece], vbuf.at[piece], in_sem.at[1, c]),
        )

    def save(c):
        piece = pl.ds(c * chunk, chunk)
        return (
            pltpu.make_async_copy(kept(0, piece), held.at[target, 0, piece], out_sem.at[0, c]),
            pltpu.make_async_copy(kept(1, piece), held.at[target, 1, piece], out_sem.at[1, c]),
        )

    def kept(which, piece):
        if arrived:
            return cache.at[0, which, piece]
        return (kbuf, vbuf)[which].at[piece]

    own_rows = pl.ds(pl.multiple_of(target * span, span), span)
    small = (
        pltpu.make_async_copy(queries.at[own_rows], qbuf, sems.at[0]),
        pltpu.make_async_copy(keys_new.at[own_rows], knbuf, sems.at[1]),
        pltpu.make_async_copy(values_new.at[own_rows], vnbuf, sems.at[2]),
    )
    weight_copy = pltpu.make_async_copy(weight, wbuf, sems.at[3])
    for copy in small:
        copy.start()
    for c in range(chunks):
        for copy in save(c) if arrived else load(c):
            copy.start()
    weight_copy.start()
    for copy in small:
        copy.wait()

    factor = HEAD**-0.5 * LOG2E
    rows = group * span
    over_head = (((1,), (1,)), ((), ()))
    over_keys = (((0,), (0,)), ((), ()))
    grouped = jnp.concatenate([qbuf[:, pl.ds(h * HEAD, HEAD)] for h in range(group)], axis=0)
    key_at = lax.broadcasted_iota(jnp.int32, (span, rows), 0)
    row_at = lax.rem(lax.broadcasted_iota(jnp.int32, (span, rows), 1), span)
    scores = lax.dot_general(knbuf[...], grouped, over_head, preferred_element_type=jnp.float32)
    scores = jnp.where(key_at <= row_at, scores * factor, MASKED)
    top = jnp.max(scores, axis=0, keepdims=True)
    weights = jnp.exp2(scores - top)
    top_ref[...] = top
    sum_ref[...] = jnp.sum(weights, axis=0, keepdims=True)
    acc[...] = lax.dot_general(
        vnbuf[...], weights.astype(jnp.bfloat16), over_keys, preferred_element_type=jnp.float32
    )

    def step(c, _):
        if not arrived:
            for copy in load(c):
                copy.wait()
            for copy in save(c):
                copy.start()

        @pl.when(c * chunk < length)
        def _():
            piece = pl.ds(pl.multiple_of(c * chunk, chunk), chunk)
            scores = lax.dot_general(kept(0, piece)[...], grouped, over_head, preferred_element_type=jnp.float32)
            seen = lax.broadcasted_iota(jnp.int32, (chunk, rows), 0) < length - c * chunk
            scores = jnp.where(seen, scores * factor, MASKED)
            before = top_ref[...]
            top = jnp.maximum(before, jnp.max(scores, axis=0, keepdims=True))
            shrink = jnp.exp2(before - top)
            weights = jnp.exp2(scores - top)
            top_ref[...] = top
            sum_ref[...] = sum_ref[...] * shrink + jnp.sum(weights, axis=0, keepdims=True)
            acc[...] = acc[...] * shrink + lax.dot_general(
                kept(1, piece)[...], weights.astype(jnp.bfloat16), over_keys, preferred_element_type=jnp.float32
            )

        return 0

    lax.fori_loop(0, chunks, step, 0)
    result = acc[...] / sum_ref[...]
    for h in range(group):
        obuf[:, pl.ds(h * HEAD, HEAD)] = result[:, h * span : (h + 1) * span].T.astype(jnp.bfloat16)
    weight_copy.wait()
    width = wbuf.shape[1] // peers
    out = 0
    for k in range(peers):
        columns = pl.ds(pl.multiple_of(lax.rem(me + k, peers) * width, width), width)
        block = jnp.dot(obuf[...], wbuf[:, columns], preferred_element_type=jnp.float32)
        block = block.astype(jnp.bfloat16)
        height = span // parts[k]
        for part in range(parts[k]):
            outs[out][...] = block[part * height : (part + 1) * height]
            out += 1
    for c in range(chunks):
        for copy in save(c):
            copy.wait()


def run_slot(lengths, moving, destination, queries, keys_new, values_new, cache, weight, parts, held=None):
    span = queries.shape[0] // lengths.shape[1]
    slots = lengths.shape[1]
    group = queries.shape[1] // HEAD
    rows = cache.shape[2]
    peers = len(parts)
    chunks = rows // CHUNK
    kept = rows if held is None else 16
    width = weight.shape[1] // peers
    smem = pl.BlockSpec(memory_space=pltpu.SMEM)
    vmem = pl.BlockSpec(memory_space=pltpu.VMEM)
    hbm = pl.BlockSpec(memory_space=pltpu.HBM)
    weight = pltpu.with_memory_space_constraint(weight, pltpu.HBM)
    if held is None:
        cache = pltpu.with_memory_space_constraint(cache, pltpu.HBM)
    operands = [lengths, moving, destination, queries, keys_new, values_new, cache, weight]
    in_specs = [smem] * 3 + [pl.BlockSpec(memory_space=pl.ANY)] * 3
    in_specs += [hbm if held is None else vmem, hbm]
    aliases = {}
    if held is not None:
        operands.append(held)
        in_specs.append(hbm)
        aliases = {8: 0}
    shapes = [jax.ShapeDtypeStruct((slots, 2, rows, HEAD), cache.dtype)]
    for count in parts:
        shapes += [jax.ShapeDtypeStruct((span // count, width), jnp.bfloat16)] * count
    flops = 4 * group * span * HEAD * (rows + span) + 2 * span * weight.shape[0] * weight.shape[1]
    return pl.pallas_call(
        functools.partial(slot_kernel, held is not None, group, CHUNK, parts),
        out_shape=shapes,
        in_specs=in_specs,
        out_specs=[hbm] + [vmem] * (len(shapes) - 1),
        scratch_shapes=[
            pltpu.VMEM((span, group * HEAD), jnp.bfloat16),
            pltpu.VMEM((span, HEAD), jnp.bfloat16),
            pltpu.VMEM((span, HEAD), jnp.bfloat16),
            pltpu.VMEM((kept, HEAD), jnp.bfloat16),
            pltpu.VMEM((kept, HEAD), jnp.bfloat16),
            pltpu.VMEM(weight.shape, jnp.bfloat16),
            pltpu.VMEM((1, group * span), jnp.float32),
            pltpu.VMEM((1, group * span), jnp.float32),
            pltpu.VMEM((HEAD, group * span), jnp.float32),
            pltpu.VMEM((span, group * HEAD), jnp.bfloat16),
            pltpu.SemaphoreType.DMA((2, chunks)),
            pltpu.SemaphoreType.DMA((2, chunks)),
            pltpu.SemaphoreType.DMA((4,)),
        ],
        input_output_aliases=aliases,
        compiler_params=pltpu.CompilerParams(vmem_limit_bytes=32 * 2**20),
        cost_estimate=pl.CostEstimate(
            flops=flops,
            bytes_accessed=8 * rows * HEAD + weight.size * 2,
            transcendentals=group * span * rows,
        ),
        name="slot",
    )(*operands)


def shift(block, k):
    peers = lax.axis_size("tp")
    return lax.ppermute(block, "tp", [(i, (i + k) % peers) for i in range(peers)])


def widen(block):
    return block.astype(jnp.float32)


def far_sums(blocks):
    b0, b1, b2, b3, b4_low, b4_high, b5, b6, b7 = blocks
    right = shift(b3, 1)
    left = shift(b5, -1)
    low = shift(b4_low, 2)
    high = shift(b4_high, -2)
    b1, b7, right, left = lax.optimization_barrier((b1, b7, right, left))
    one = shift(b1, 1)
    seven = shift(b7, -1)
    none = jnp.zeros_like(low)
    right = widen(b2) + widen(right) + widen(jnp.concatenate([low, none]))
    left = widen(b6) + widen(left) + widen(jnp.concatenate([none, high]))
    return b0, one, seven, right.astype(jnp.bfloat16), left.astype(jnp.bfloat16)


def owner_sum(b0, one, seven, right, left):
    return widen(b0) + widen(one) + widen(seven) + widen(shift(right, 2)) + widen(shift(left, -2))


def on_device(queries, keys_new, values_new, caches, lengths, moving, destination, out_weight):
    replicas = lax.axis_size(REP)
    peers = lax.axis_size("tp")
    slots, _, rows, _ = caches.shape
    span = queries.shape[0] // slots
    order = jnp.arange(replicas, dtype=jnp.int32)
    source_of = jnp.sum(jnp.where(destination[None, :] == order[:, None], order[None, :], 0), axis=1)
    small = (lengths, moving, destination, queries, keys_new, values_new)

    sent = pick(moving, caches).reshape(replicas, 2 * rows // replicas, HEAD)
    spread = lax.all_to_all(sent, REP, 0, 0, tiled=True)
    held, *stay = run_slot(*small, caches, out_weight, PARTS)
    stay = far_sums(stay)
    spread, stay = lax.optimization_barrier((spread, stay))
    ordered = spread.at[source_of].get(mode="promise_in_bounds")
    arrived = lax.all_to_all(ordered, REP, 0, 0, tiled=True)
    stay_mixed = owner_sum(*stay).astype(jnp.bfloat16)

    leaving = moving[lax.axis_index(REP)]
    own = lax.broadcasted_iota(jnp.int32, (slots, 1, 1), 0) == leaving
    arrived, stay_mixed, own = lax.optimization_barrier((arrived, stay_mixed, own))
    arrived = arrived.reshape(1, 2, rows, HEAD)
    held, *move = run_slot(*small, arrived, out_weight, PARTS, held)
    move_mixed = owner_sum(*far_sums(move)).astype(jnp.bfloat16)
    mixed = jnp.where(own, move_mixed[None], stay_mixed[None])
    return mixed.reshape(slots * span, -1), held


def solution(mesh):
    split = Mesh(mesh.devices.reshape(4, 4, 2, mesh.shape["tp"]), REP + ("tp",))
    return jax.shard_map(
        on_device,
        mesh=split,
        in_specs=(
            P(REP, "tp"),
            P(REP, "tp"),
            P(REP, "tp"),
            P(REP, None, None, "tp"),
            P(),
            P(),
            P(),
            P("tp", None),
        ),
        out_specs=(P(REP, "tp"), P(REP, None, None, "tp")),
        check_vma=False,
    )
```

```python
import functools

import jax
import jax.numpy as jnp
from jax import lax
from jax.experimental import pallas as pl
from jax.experimental.pallas import tpu as pltpu
from jax.sharding import Mesh
from jax.sharding import PartitionSpec as P

HEAD = 128
REP = ("rep_0", "rep_1", "rep_2")
LOG2E = 1.4426950408889634
MASKED = -1e30
CHUNK = 2048
PARTS = (1, 1, 1, 1, 2, 1, 1, 1)


def place():
    return lax.axis_index(REP).astype(jnp.int32), lax.axis_index("tp").astype(jnp.int32)


def pick_kernel(moving, caches, sent, held, in_sems, out_sems):
    own, _ = place()
    leaving = moving[own]
    pieces = in_sems.shape[0]
    rows = sent.shape[0] // pieces

    def load(i):
        piece = pl.ds(i * rows, rows)
        return pltpu.make_async_copy(caches.at[leaving, piece], held.at[piece], in_sems.at[i])

    def save(i):
        piece = pl.ds(i * rows, rows)
        return pltpu.make_async_copy(held.at[piece], sent.at[piece], out_sems.at[i])

    for i in range(pieces):
        load(i).start()
    for i in range(pieces):
        load(i).wait()
        save(i).start()
    for i in range(pieces):
        save(i).wait()


def pick(moving, caches):
    slots, _, rows, _ = caches.shape
    hbm = pl.BlockSpec(memory_space=pltpu.HBM)
    caches = pltpu.with_memory_space_constraint(caches.reshape(slots, 2 * rows, HEAD), pltpu.HBM)
    return pl.pallas_call(
        pick_kernel,
        out_shape=jax.ShapeDtypeStruct((2 * rows, HEAD), caches.dtype),
        in_specs=[pl.BlockSpec(memory_space=pltpu.SMEM), hbm],
        out_specs=hbm,
        scratch_shapes=[
            pltpu.VMEM((2 * rows, HEAD), caches.dtype),
            pltpu.SemaphoreType.DMA((8,)),
            pltpu.SemaphoreType.DMA((8,)),
        ],
        compiler_params=pltpu.CompilerParams(vmem_limit_bytes=60 * 2**20),
        cost_estimate=pl.CostEstimate(flops=0, bytes_accessed=8 * rows * HEAD, transcendentals=0),
        name="pick",
    )(moving, caches)


def slot_kernel(arrived, group, chunk, parts, lengths, moving, destination, queries, keys_new, values_new, cache, weight, *rest):
    scratch = 10
    if arrived:
        rest = rest[1:]
    held = rest[0]
    outs = rest[1:-scratch]
    (kbuf, vbuf, wbuf, top_ref, sum_ref, acc, obuf, in_sem, out_sem, sems) = rest[-scratch:]
    own, me = place()
    replicas = destination.shape[0]
    chunks = cache.shape[2] // chunk
    span = obuf.shape[0]
    peers = len(parts)
    leaving = moving[own]
    if arrived:
        source, target = 0, leaving
        anchor = jnp.int32(0)
        for r in range(replicas):
            anchor = jnp.where(destination[r] == own, r, anchor)
        length = lengths[anchor, moving[anchor]]
    else:
        source = target = 1 - leaving
        length = lengths[own, target]

    def load(c):
        piece = pl.ds(c * chunk, chunk)
        return (
            pltpu.make_async_copy(cache.at[source, 0, piece], kbuf.at[piece], in_sem.at[0, c]),
            pltpu.make_async_copy(cache.at[source, 1, piece], vbuf.at[piece], in_sem.at[1, c]),
        )

    def save(c):
        piece = pl.ds(c * chunk, chunk)
        return (
            pltpu.make_async_copy(kept(0, piece), held.at[target, 0, piece], out_sem.at[0, c]),
            pltpu.make_async_copy(kept(1, piece), held.at[target, 1, piece], out_sem.at[1, c]),
        )

    def kept(which, piece):
        if arrived:
            return cache.at[0, which, piece]
        return (kbuf, vbuf)[which].at[piece]

    own_rows = pl.ds(pl.multiple_of(target * span, span), span)
    weight_copy = pltpu.make_async_copy(weight, wbuf, sems.at[3])
    for c in range(chunks):
        for copy in save(c) if arrived else load(c):
            copy.start()
    weight_copy.start()

    factor = HEAD**-0.5 * LOG2E
    rows = group * span
    over_head = (((1,), (1,)), ((), ()))
    over_keys = (((0,), (0,)), ((), ()))
    grouped = jnp.concatenate([queries[own_rows, pl.ds(h * HEAD, HEAD)] for h in range(group)], axis=0)
    key_at = lax.broadcasted_iota(jnp.int32, (span, rows), 0)
    row_at = lax.rem(lax.broadcasted_iota(jnp.int32, (span, rows), 1), span)
    scores = lax.dot_general(keys_new[own_rows, :], grouped, over_head, preferred_element_type=jnp.float32)
    scores = jnp.where(key_at <= row_at, scores * factor, MASKED)
    top = jnp.max(scores, axis=0, keepdims=True)
    weights = jnp.exp2(scores - top)
    top_ref[...] = top
    sum_ref[...] = jnp.sum(weights, axis=0, keepdims=True)
    acc[...] = lax.dot_general(
        values_new[own_rows, :], weights.astype(jnp.bfloat16), over_keys, preferred_element_type=jnp.float32
    )

    def step(c, _):
        if not arrived:
            for copy in load(c):
                copy.wait()
            for copy in save(c):
                copy.start()

        @pl.when(c * chunk < length)
        def _():
            piece = pl.ds(pl.multiple_of(c * chunk, chunk), chunk)
            scores = lax.dot_general(kept(0, piece)[...], grouped, over_head, preferred_element_type=jnp.float32)
            seen = lax.broadcasted_iota(jnp.int32, (chunk, rows), 0) < length - c * chunk
            scores = jnp.where(seen, scores * factor, MASKED)
            before = top_ref[...]
            top = jnp.maximum(before, jnp.max(scores, axis=0, keepdims=True))
            shrink = jnp.exp2(before - top)
            weights = jnp.exp2(scores - top)
            top_ref[...] = top
            sum_ref[...] = sum_ref[...] * shrink + jnp.sum(weights, axis=0, keepdims=True)
            acc[...] = acc[...] * shrink + lax.dot_general(
                kept(1, piece)[...], weights.astype(jnp.bfloat16), over_keys, preferred_element_type=jnp.float32
            )

        return 0

    lax.fori_loop(0, chunks, step, 0)
    result = acc[...] / sum_ref[...]
    for h in range(group):
        obuf[:, pl.ds(h * HEAD, HEAD)] = result[:, h * span : (h + 1) * span].T.astype(jnp.bfloat16)
    weight_copy.wait()
    width = wbuf.shape[1] // peers
    out = 0
    for k in range(peers):
        columns = pl.ds(pl.multiple_of(lax.rem(me + k, peers) * width, width), width)
        block = jnp.dot(obuf[...], wbuf[:, columns], preferred_element_type=jnp.float32)
        block = block.astype(jnp.bfloat16)
        height = span // parts[k]
        for part in range(parts[k]):
            outs[out][...] = block[part * height : (part + 1) * height]
            out += 1
    for c in range(chunks):
        for copy in save(c):
            copy.wait()


def run_slot(lengths, moving, destination, queries, keys_new, values_new, cache, weight, parts, held=None):
    span = queries.shape[0] // lengths.shape[1]
    slots = lengths.shape[1]
    group = queries.shape[1] // HEAD
    rows = cache.shape[2]
    peers = len(parts)
    chunks = rows // CHUNK
    kept = rows if held is None else 16
    width = weight.shape[1] // peers
    smem = pl.BlockSpec(memory_space=pltpu.SMEM)
    vmem = pl.BlockSpec(memory_space=pltpu.VMEM)
    hbm = pl.BlockSpec(memory_space=pltpu.HBM)
    weight = pltpu.with_memory_space_constraint(weight, pltpu.HBM)
    if held is None:
        cache = pltpu.with_memory_space_constraint(cache, pltpu.HBM)
    operands = [lengths, moving, destination, queries, keys_new, values_new, cache, weight]
    in_specs = [smem] * 3 + [vmem] * 3
    in_specs += [hbm if held is None else vmem, hbm]
    aliases = {}
    if held is not None:
        operands.append(held)
        in_specs.append(hbm)
        aliases = {8: 0}
    shapes = [jax.ShapeDtypeStruct((slots, 2, rows, HEAD), cache.dtype)]
    for count in parts:
        shapes += [jax.ShapeDtypeStruct((span // count, width), jnp.bfloat16)] * count
    flops = 4 * group * span * HEAD * (rows + span) + 2 * span * weight.shape[0] * weight.shape[1]
    return pl.pallas_call(
        functools.partial(slot_kernel, held is not None, group, CHUNK, parts),
        out_shape=shapes,
        in_specs=in_specs,
        out_specs=[hbm] + [vmem] * (len(shapes) - 1),
        scratch_shapes=[
            pltpu.VMEM((kept, HEAD), jnp.bfloat16),
            pltpu.VMEM((kept, HEAD), jnp.bfloat16),
            pltpu.VMEM(weight.shape, jnp.bfloat16),
            pltpu.VMEM((1, group * span), jnp.float32),
            pltpu.VMEM((1, group * span), jnp.float32),
            pltpu.VMEM((HEAD, group * span), jnp.float32),
            pltpu.VMEM((span, group * HEAD), jnp.bfloat16),
            pltpu.SemaphoreType.DMA((2, chunks)),
            pltpu.SemaphoreType.DMA((2, chunks)),
            pltpu.SemaphoreType.DMA((4,)),
        ],
        input_output_aliases=aliases,
        compiler_params=pltpu.CompilerParams(vmem_limit_bytes=32 * 2**20),
        cost_estimate=pl.CostEstimate(
            flops=flops,
            bytes_accessed=8 * rows * HEAD + weight.size * 2,
            transcendentals=group * span * rows,
        ),
        name="slot",
    )(*operands)


def shift(block, k):
    peers = lax.axis_size("tp")
    return lax.ppermute(block, "tp", [(i, (i + k) % peers) for i in range(peers)])


def widen(block):
    return block.astype(jnp.float32)


def far_sums(blocks):
    b0, b1, b2, b3, b4_low, b4_high, b5, b6, b7 = blocks
    right = shift(b3, 1)
    left = shift(b5, -1)
    low = shift(b4_low, 2)
    high = shift(b4_high, -2)
    one = shift(b1, 1)
    seven = shift(b7, -1)
    none = jnp.zeros_like(low)
    right = widen(b2) + widen(right) + widen(jnp.concatenate([low, none]))
    left = widen(b6) + widen(left) + widen(jnp.concatenate([none, high]))
    return b0, one, seven, right.astype(jnp.bfloat16), left.astype(jnp.bfloat16)


def owner_sum(b0, one, seven, right, left):
    two = shift(right, 2)
    six = shift(left, -2)
    return widen(b0) + widen(one) + widen(seven) + widen(two) + widen(six)


def on_device(queries, keys_new, values_new, caches, lengths, moving, destination, out_weight):
    replicas = lax.axis_size(REP)
    slots, _, rows, _ = caches.shape
    span = queries.shape[0] // slots
    order = jnp.arange(replicas, dtype=jnp.int32)
    source_of = jnp.sum(jnp.where(destination[None, :] == order[:, None], order[None, :], 0), axis=1)
    small = (lengths, moving, destination, queries, keys_new, values_new)

    sent = pick(moving, caches).reshape(replicas, 2 * rows // replicas, HEAD)
    spread = lax.all_to_all(sent, REP, 0, 0, tiled=True)
    held, *stay = run_slot(*small, caches, out_weight, PARTS)
    stay = far_sums(stay)
    spread, stay = lax.optimization_barrier((spread, stay))
    ordered = spread.at[source_of].get(mode="promise_in_bounds")
    arrived = lax.all_to_all(ordered, REP, 0, 0, tiled=True)
    stay_mixed = owner_sum(*stay).astype(jnp.bfloat16)

    leaving = moving[lax.axis_index(REP)]
    own = lax.broadcasted_iota(jnp.int32, (slots, 1, 1), 0) == leaving
    arrived, stay_mixed, own = lax.optimization_barrier((arrived, stay_mixed, own))
    arrived = arrived.reshape(1, 2, rows, HEAD)
    held, *move = run_slot(*small, arrived, out_weight, PARTS, held)
    move_mixed = owner_sum(*far_sums(move)).astype(jnp.bfloat16)
    mixed = jnp.where(own, move_mixed[None], stay_mixed[None])
    return mixed.reshape(slots * span, -1), held


def solution(mesh):
    split = Mesh(mesh.devices.reshape(4, 4, 2, mesh.shape["tp"]), REP + ("tp",))
    return jax.shard_map(
        on_device,
        mesh=split,
        in_specs=(
            P(REP, "tp"),
            P(REP, "tp"),
            P(REP, "tp"),
            P(REP, None, None, "tp"),
            P(),
            P(),
            P(),
            P("tp", None),
        ),
        out_specs=(P(REP, "tp"), P(REP, None, None, "tp")),
        check_vma=False,
    )
```

```python
import functools

import jax
import jax.numpy as jnp
from jax import lax
from jax.experimental import pallas as pl
from jax.experimental.pallas import tpu as pltpu
from jax.sharding import Mesh
from jax.sharding import PartitionSpec as P

HEAD = 128
REP = ("rep_0", "rep_1", "rep_2")
LOG2E = 1.4426950408889634
MASKED = -1e30
CHUNK = 2048
PARTS = (1, 1, 1, 1, 2, 1, 1, 1)


def place():
    return lax.axis_index(REP).astype(jnp.int32), lax.axis_index("tp").astype(jnp.int32)


def pick_kernel(moving, caches, sent, held, in_sems, out_sems):
    own, _ = place()
    leaving = moving[own]
    pieces = in_sems.shape[0]
    rows = sent.shape[0] // pieces

    def load(i):
        piece = pl.ds(i * rows, rows)
        return pltpu.make_async_copy(caches.at[leaving, piece], held.at[piece], in_sems.at[i])

    def save(i):
        piece = pl.ds(i * rows, rows)
        return pltpu.make_async_copy(held.at[piece], sent.at[piece], out_sems.at[i])

    for i in range(pieces):
        load(i).start()
    for i in range(pieces):
        load(i).wait()
        save(i).start()
    for i in range(pieces):
        save(i).wait()


def pick(moving, caches):
    slots, _, rows, _ = caches.shape
    hbm = pl.BlockSpec(memory_space=pltpu.HBM)
    caches = pltpu.with_memory_space_constraint(caches.reshape(slots, 2 * rows, HEAD), pltpu.HBM)
    return pl.pallas_call(
        pick_kernel,
        out_shape=jax.ShapeDtypeStruct((2 * rows, HEAD), caches.dtype),
        in_specs=[pl.BlockSpec(memory_space=pltpu.SMEM), hbm],
        out_specs=hbm,
        scratch_shapes=[
            pltpu.VMEM((2 * rows, HEAD), caches.dtype),
            pltpu.SemaphoreType.DMA((8,)),
            pltpu.SemaphoreType.DMA((8,)),
        ],
        compiler_params=pltpu.CompilerParams(vmem_limit_bytes=60 * 2**20),
        cost_estimate=pl.CostEstimate(flops=0, bytes_accessed=8 * rows * HEAD, transcendentals=0),
        name="pick",
    )(moving, caches)


def slot_kernel(arrived, group, chunk, parts, lengths, moving, destination, queries, keys_new, values_new, cache, weight, *rest):
    scratch = 10
    if arrived:
        rest = rest[1:]
    held = rest[0]
    outs = rest[1:-scratch]
    (kbuf, vbuf, wbuf, top_ref, sum_ref, acc, obuf, in_sem, out_sem, sems) = rest[-scratch:]
    own, me = place()
    replicas = destination.shape[0]
    chunks = cache.shape[2] // chunk
    span = obuf.shape[0]
    peers = len(parts)
    leaving = moving[own]
    if arrived:
        source, target = 0, leaving
        anchor = jnp.int32(0)
        for r in range(replicas):
            anchor = jnp.where(destination[r] == own, r, anchor)
        length = lengths[anchor, moving[anchor]]
    else:
        source = target = 1 - leaving
        length = lengths[own, target]

    def load(c):
        piece = pl.ds(c * chunk, chunk)
        return (
            pltpu.make_async_copy(cache.at[source, 0, piece], kbuf.at[piece], in_sem.at[0, c]),
            pltpu.make_async_copy(cache.at[source, 1, piece], vbuf.at[piece], in_sem.at[1, c]),
        )

    def save(c):
        piece = pl.ds(c * chunk, chunk)
        return (
            pltpu.make_async_copy(kept(0, piece), held.at[target, 0, piece], out_sem.at[0, c]),
            pltpu.make_async_copy(kept(1, piece), held.at[target, 1, piece], out_sem.at[1, c]),
        )

    def kept(which, piece):
        if arrived:
            return cache.at[0, which, piece]
        return (kbuf, vbuf)[which].at[piece]

    own_rows = pl.ds(pl.multiple_of(target * span, span), span)
    weight_copy = pltpu.make_async_copy(weight, wbuf, sems.at[3])
    for c in range(chunks):
        for copy in save(c) if arrived else load(c):
            copy.start()
    weight_copy.start()

    factor = HEAD**-0.5 * LOG2E
    rows = group * span
    over_head = (((1,), (1,)), ((), ()))
    over_keys = (((0,), (0,)), ((), ()))
    grouped = jnp.concatenate([queries[own_rows, pl.ds(h * HEAD, HEAD)] for h in range(group)], axis=0)
    key_at = lax.broadcasted_iota(jnp.int32, (span, rows), 0)
    row_at = lax.rem(lax.broadcasted_iota(jnp.int32, (span, rows), 1), span)
    scores = lax.dot_general(keys_new[own_rows, :], grouped, over_head, preferred_element_type=jnp.float32)
    scores = jnp.where(key_at <= row_at, scores * factor, MASKED)
    top = jnp.max(scores, axis=0, keepdims=True)
    weights = jnp.exp2(scores - top)
    top_ref[...] = top
    sum_ref[...] = jnp.sum(weights, axis=0, keepdims=True)
    acc[...] = lax.dot_general(
        values_new[own_rows, :], weights.astype(jnp.bfloat16), over_keys, preferred_element_type=jnp.float32
    )

    def step(c, _):
        if not arrived:
            for copy in load(c):
                copy.wait()
            for copy in save(c):
                copy.start()

        def absorb(partly):
            piece = pl.ds(pl.multiple_of(c * chunk, chunk), chunk)
            scores = lax.dot_general(kept(0, piece)[...], grouped, over_head, preferred_element_type=jnp.float32)
            scores = scores * factor
            if partly:
                seen = lax.broadcasted_iota(jnp.int32, (chunk, rows), 0) < length - c * chunk
                scores = jnp.where(seen, scores, MASKED)
            before = top_ref[...]
            top = jnp.maximum(before, jnp.max(scores, axis=0, keepdims=True))
            shrink = jnp.exp2(before - top)
            weights = jnp.exp2(scores - top)
            top_ref[...] = top
            sum_ref[...] = sum_ref[...] * shrink + jnp.sum(weights, axis=0, keepdims=True)
            acc[...] = acc[...] * shrink + lax.dot_general(
                kept(1, piece)[...], weights.astype(jnp.bfloat16), over_keys, preferred_element_type=jnp.float32
            )

        whole = (c + 1) * chunk <= length
        pl.when(whole)(functools.partial(absorb, False))
        pl.when(jnp.logical_and(c * chunk < length, jnp.logical_not(whole)))(functools.partial(absorb, True))
        return 0

    lax.fori_loop(0, chunks, step, 0)
    result = acc[...] / sum_ref[...]
    for h in range(group):
        obuf[:, pl.ds(h * HEAD, HEAD)] = result[:, h * span : (h + 1) * span].T.astype(jnp.bfloat16)
    weight_copy.wait()
    width = wbuf.shape[1] // peers
    out = 0
    for k in range(peers):
        owner = lax.rem(me + jnp.where(lax.rem(own, 2) == 0, k, peers - k), peers)
        columns = pl.ds(pl.multiple_of(owner * width, width), width)
        block = jnp.dot(obuf[...], wbuf[:, columns], preferred_element_type=jnp.float32)
        block = block.astype(jnp.bfloat16)
        height = span // parts[k]
        for part in range(parts[k]):
            outs[out][...] = block[part * height : (part + 1) * height]
            out += 1
    for c in range(chunks):
        for copy in save(c):
            copy.wait()


def run_slot(lengths, moving, destination, queries, keys_new, values_new, cache, weight, parts, held=None):
    span = queries.shape[0] // lengths.shape[1]
    slots = lengths.shape[1]
    group = queries.shape[1] // HEAD
    rows = cache.shape[2]
    peers = len(parts)
    chunks = rows // CHUNK
    kept = rows if held is None else 16
    width = weight.shape[1] // peers
    smem = pl.BlockSpec(memory_space=pltpu.SMEM)
    vmem = pl.BlockSpec(memory_space=pltpu.VMEM)
    hbm = pl.BlockSpec(memory_space=pltpu.HBM)
    weight = pltpu.with_memory_space_constraint(weight, pltpu.HBM)
    if held is None:
        cache = pltpu.with_memory_space_constraint(cache, pltpu.HBM)
    operands = [lengths, moving, destination, queries, keys_new, values_new, cache, weight]
    in_specs = [smem] * 3 + [vmem] * 3
    in_specs += [hbm if held is None else vmem, hbm]
    aliases = {}
    if held is not None:
        operands.append(held)
        in_specs.append(hbm)
        aliases = {8: 0}
    shapes = [jax.ShapeDtypeStruct((slots, 2, rows, HEAD), cache.dtype)]
    for count in parts:
        shapes += [jax.ShapeDtypeStruct((span // count, width), jnp.bfloat16)] * count
    flops = 4 * group * span * HEAD * (rows + span) + 2 * span * weight.shape[0] * weight.shape[1]
    return pl.pallas_call(
        functools.partial(slot_kernel, held is not None, group, CHUNK, parts),
        out_shape=shapes,
        in_specs=in_specs,
        out_specs=[hbm] + [vmem] * (len(shapes) - 1),
        scratch_shapes=[
            pltpu.VMEM((kept, HEAD), jnp.bfloat16),
            pltpu.VMEM((kept, HEAD), jnp.bfloat16),
            pltpu.VMEM(weight.shape, jnp.bfloat16),
            pltpu.VMEM((1, group * span), jnp.float32),
            pltpu.VMEM((1, group * span), jnp.float32),
            pltpu.VMEM((HEAD, group * span), jnp.float32),
            pltpu.VMEM((span, group * HEAD), jnp.bfloat16),
            pltpu.SemaphoreType.DMA((2, chunks)),
            pltpu.SemaphoreType.DMA((2, chunks)),
            pltpu.SemaphoreType.DMA((4,)),
        ],
        input_output_aliases=aliases,
        compiler_params=pltpu.CompilerParams(vmem_limit_bytes=32 * 2**20),
        cost_estimate=pl.CostEstimate(
            flops=flops,
            bytes_accessed=8 * rows * HEAD + weight.size * 2,
            transcendentals=group * span * rows,
        ),
        name="slot",
    )(*operands)


def shift(block, k):
    peers = lax.axis_size("tp")
    pairs = [(i, (i + k) % peers) for i in range(peers)]
    pairs += [(peers + i, peers + (i - k) % peers) for i in range(peers)]
    return lax.ppermute(block, ("rep_2", "tp"), pairs)


def widen(block):
    return block.astype(jnp.float32)


def far_sums(blocks):
    b0, b1, b2, b3, b4_low, b4_high, b5, b6, b7 = blocks
    right = shift(b3, 1)
    left = shift(b5, -1)
    low = shift(b4_low, 2)
    high = shift(b4_high, -2)
    one = shift(b1, 1)
    seven = shift(b7, -1)
    none = jnp.zeros_like(low)
    right = widen(b2) + widen(right) + widen(jnp.concatenate([low, none]))
    left = widen(b6) + widen(left) + widen(jnp.concatenate([none, high]))
    return b0, one, seven, right.astype(jnp.bfloat16), left.astype(jnp.bfloat16)


def owner_sum(b0, one, seven, right, left):
    two = shift(right, 2)
    six = shift(left, -2)
    return widen(b0) + widen(one) + widen(seven) + widen(two) + widen(six)


def on_device(queries, keys_new, values_new, caches, lengths, moving, destination, out_weight):
    replicas = lax.axis_size(REP)
    slots, _, rows, _ = caches.shape
    span = queries.shape[0] // slots
    order = jnp.arange(replicas, dtype=jnp.int32)
    source_of = jnp.sum(jnp.where(destination[None, :] == order[:, None], order[None, :], 0), axis=1)
    small = (lengths, moving, destination, queries, keys_new, values_new)

    sent = pick(moving, caches).reshape(replicas, 2 * rows // replicas, HEAD)
    spread = lax.all_to_all(sent, REP, 0, 0, tiled=True)
    held, *stay = run_slot(*small, caches, out_weight, PARTS)
    stay = far_sums(stay)
    spread, stay = lax.optimization_barrier((spread, stay))
    ordered = spread.at[source_of].get(mode="promise_in_bounds")
    arrived = lax.all_to_all(ordered, REP, 0, 0, tiled=True)
    stay_mixed = owner_sum(*stay).astype(jnp.bfloat16)

    leaving = moving[lax.axis_index(REP)]
    own = lax.broadcasted_iota(jnp.int32, (slots, 1, 1), 0) == leaving
    arrived, stay_mixed, own = lax.optimization_barrier((arrived, stay_mixed, own))
    arrived = arrived.reshape(1, 2, rows, HEAD)
    held, *move = run_slot(*small, arrived, out_weight, PARTS, held)
    move_mixed = owner_sum(*far_sums(move)).astype(jnp.bfloat16)
    mixed = jnp.where(own, move_mixed[None], stay_mixed[None])
    return mixed.reshape(slots * span, -1), held


def solution(mesh):
    split = Mesh(mesh.devices.reshape(4, 4, 2, mesh.shape["tp"]), REP + ("tp",))
    return jax.shard_map(
        on_device,
        mesh=split,
        in_specs=(
            P(REP, "tp"),
            P(REP, "tp"),
            P(REP, "tp"),
            P(REP, None, None, "tp"),
            P(),
            P(),
            P(),
            P("tp", None),
        ),
        out_specs=(P(REP, "tp"), P(REP, None, None, "tp")),
        check_vma=False,
    )
```
